32 devices in a mesh: row: 4 (over z), col: 8 (over y, x, core).
Axes of the slice: x: 2, y: 2, z: 4, core: 2. Of those that a mesh axis runs over, the one named last changes fastest.
Arguments:
- kernel: bfloat16 [16384, 16384], P('row', 'col'), may hold values from -6 to 6
- labels: int32 [3, 16384], replicated, may hold values from 0 to 63, as said below
Outputs:
- distance: float32 [3, 16384, 64], P(None, ('row', 'col'))
- objective: float32 [3], replicated
The draws below stay inside these ranges and needn't reach their ends.
Inputs may be any that keep to these rules, and one draw needn't show every extreme that they name: `labels`: in every iteration every cluster of 0 to 63 is named by at least one series.
All inputs are finite; a program needn't handle non-finite values.
Results may differ from the reference program's by a relative error of at most 0.0003.
Values sent between devices are 32-bit elements; how exact they have to be, the bound alone decides.
A program may use at most 64 MiB of HBM per device.

```python
import jax
import jax.numpy as jnp

SERIES = 16384
CLUSTERS = 64
ITERS = 3


def draw_labels(key, part):
    rows = []
    for step in range(ITERS):
        folded = jax.random.fold_in(key, 7919 + step)
        first, second, third, fourth = jax.random.split(folded, 4)
        drawn = jax.random.randint(first, (SERIES,), 0, CLUSTERS)
        other = jax.random.randint(second, (SERIES,), 0, CLUSTERS)
        pick = jax.random.randint(third, (SERIES,), 0, 2)
        chosen = jnp.where(pick == 1, jnp.minimum(drawn, other), drawn)
        places = jax.random.permutation(fourth, SERIES)[:CLUSTERS]
        chosen = chosen.at[places].set(jnp.arange(CLUSTERS, dtype=jnp.int32))
        rows.append(chosen.astype(jnp.int32))
    return jnp.stack(rows)


def with_spikes(array, key, source, target, blocks, factor):
    owner, partner = [(jnp.arange(array.shape[position]) // (array.shape[position] // blocks)).reshape([-1 if axis == position else 1 for axis in range(array.ndim)]) for position in (source, target)]
    chosen = jax.random.permutation(key, blocks)[partner]
    strong = (owner == chosen) | (owner == (partner + blocks // 2) % blocks)
    return jnp.where(strong, factor * array, array)


def level_of(rng, extent, cuts, smallest, largest):
    gain, own = 1.0, jax.random.fold_in(rng, 6)
    for axis_at, shards_of in cuts:
        steps = jnp.exp(jax.random.uniform(jax.random.fold_in(own, axis_at), (shards_of,), jnp.float32, smallest / len(cuts), largest / len(cuts)))
        gain = gain * jnp.repeat(steps, extent[axis_at] // shards_of).reshape([-1 if axis == axis_at else 1 for axis in range(len(extent))])
    return gain


def bell_draw_with(own_key, shape, scale, most, pieces, heavy, held_as=jnp.bfloat16):
    array = scale * jax.random.normal(own_key, shape, jnp.float32)
    if pieces:
        array = array * level_of(own_key, shape, pieces, -0.22, 0.18)
    return jnp.clip(with_spikes(array, jax.random.fold_in(own_key, 3), *heavy), -most, most).astype(held_as)


def setup_inputs(seed: int = 0) -> dict:
    arg_keys = jax.random.split(jax.random.key(seed), 3)
    return {
        "kernel": bell_draw_with(arg_keys[0], (SERIES, SERIES), 1.0, 6.0, ((0, 4), (1, 8)), (1, 0, 8, 2.0)),
        "labels": draw_labels(jax.random.fold_in(arg_keys[2], 71), 0),
    }


def reference(kernel, labels):
    clusters = jnp.arange(CLUSTERS, dtype=jnp.int32)
    dists = []
    objs = []
    for step in range(ITERS):
        onehot = (labels[step][:, None] == clusters[None, :]).astype(jnp.bfloat16)
        sums = jnp.dot(kernel, onehot, preferred_element_type=jnp.float32)
        weights = onehot.astype(jnp.float32)
        counts = jnp.sum(weights, axis=0)
        totals = jnp.sum(weights * sums, axis=0)
        dists.append((-2.0 * sums) / counts[None, :] + totals[None, :] / (counts * counts)[None, :])
        objs.append(1.0 - jnp.sum(totals / counts) / SERIES)
    return jnp.stack(dists), jnp.stack(objs)
```

```python
import functools

import jax
import jax.numpy as jnp
from jax import lax
from jax.experimental import pallas as pl
from jax.experimental.pallas import tpu as pltpu
from jax.sharding import PartitionSpec as P

CLUSTERS = 64
LANES = 128
SPLITS = 2
LAG = 1
MESH = pl.DeviceIdType.MESH


def flip(index, mask, bits):
    out = 0
    for b in range(bits):
        bit = lax.rem(lax.div(index, 1 << b), 2)
        if mask >> b & 1:
            bit = 1 - bit
        out = out + bit * (1 << b)
    return out


def body(n, rows, iters, series, k_hbm, lab_hbm, dist_ref, obj_ref,
         kbuf, labc, labr, oh, acc, rcv, tot, tot_col, tot_sum, tot_row,
         k_sem, lab_sem, send_sem, recv_sem, tsend, trecv, rsend, rrecv):
    bits = n.bit_length() - 1
    pr = kbuf.shape[2]
    half = pr // 2
    cols = kbuf.shape[3]
    slice_rows = SPLITS * pr
    row = lax.axis_index("row")
    me = lax.axis_index("col")
    peers = [flip(me, r, bits) for r in range(n)]
    lanes = []
    for s in range(SPLITS):
        rest = list(range(1, bits))
        lanes.append(rest if s % 2 == 0 else rest[::-1])

    def first(r, s):
        hits = [k for k, b in enumerate(lanes[s]) if r >> b & 1]
        return hits[0] if hits else bits

    items = [(r, s) for r in range(0, n, 2) for s in range(SPLITS)]
    items.sort(key=lambda rs: (first(*rs), -bin(rs[0]).count("1"), rs[1]))

    slots = {}
    for s in range(SPLITS):
        gone = 0
        for b in [0] + lanes[s]:
            gone |= 1 << b
            for r in range(n):
                if r & gone == 0:
                    slots[b, r, s] = len(slots)

    lab_copies = [pltpu.make_async_copy(
        lab_hbm.at[:, pl.ds(pl.multiple_of(me * cols, LANES), cols)], labc, lab_sem.at[n])]
    lab_copies[0].start()
    k_copies = {}

    def fetch(r, s):
        base = row * (n * slice_rows) + peers[r] * slice_rows
        start = peers[r] * slice_rows + s * pr
        k_copies[r, s] = pltpu.make_async_copy(
            k_hbm.at[pl.ds(pl.multiple_of(start, 16), pr), :], kbuf.at[r, s], k_sem.at[r, s])
        k_copies[r, s].start()
        if s == 0:
            c = pltpu.make_async_copy(
                lab_hbm.at[:, pl.ds(pl.multiple_of(base, LANES), slice_rows)], labr.at[r], lab_sem.at[r])
            c.start()
            lab_copies.append(c)

    for r, s in items:
        fetch(r | 1, s)
        fetch(r, s)

    barrier = pltpu.get_barrier_semaphore()
    for r in range(1, n):
        pl.semaphore_signal(barrier, inc=1, device_id=(row, peers[r]), device_id_type=MESH)
    for d in range(1, rows):
        pl.semaphore_signal(barrier, inc=1, device_id=(lax.rem(row + d, rows), me), device_id_type=MESH)

    for c in lab_copies:
        c.wait()
    width = oh.shape[1]
    step = 256
    for kb in range(cols // step):
        lab = labc[:, pl.ds(kb * step, step)]
        ids = lax.broadcasted_iota(jnp.int32, (CLUSTERS, step), 0)
        parts = [(ids == lab[t:t + 1, :]).astype(jnp.float32) for t in range(iters)]
        parts.append(jnp.zeros((width - iters * CLUSTERS, step), jnp.float32))
        oh[pl.ds(kb * step, step), :] = jnp.concatenate(parts, axis=0).T.astype(jnp.bfloat16)

    lane = lax.broadcasted_iota(jnp.int32, (pr, LANES), 1)
    low = lane < CLUSTERS
    cluster = jnp.where(low, lane, lane - CLUSTERS)
    totals = [jnp.zeros((8, LANES), jnp.float32) for _ in range(2)]

    def piece(r, s):
        k_copies[r, s].wait()
        out = jnp.dot(kbuf[r, s], oh[...], preferred_element_type=jnp.float32)
        front, back = out[:, :LANES], out[:, LANES:]
        back = jnp.where(low[:half], back[:half], pltpu.roll(back[half:], CLUSTERS, 1))
        acc[r, s, :pr, :] = front
        acc[r, s, pr:, :] = back
        lab = labr[r].T[s * pr:(s + 1) * pr, :]
        mine = jnp.where(low, lab[:, 0:1], lab[:, 1:2]) == cluster
        totals[0] += jnp.sum(jnp.where(mine, front, 0.0).reshape(pr // 8, 8, LANES), axis=0)
        mine = jnp.where(low[:half], lab[:half, 2:3], lab[half:, 2:3]) == cluster[:half]
        totals[1] += jnp.sum(jnp.where(mine, back, 0.0).reshape(half // 8, 8, LANES), axis=0)

    copies = {}

    def exchange(b, r, s):
        i = slots[b, r & ~(1 << b), s]
        c = pltpu.make_async_remote_copy(
            src_ref=acc.at[r, s], dst_ref=rcv.at[i], send_sem=send_sem.at[i], recv_sem=recv_sem.at[i],
            device_id=(row, peers[1 << b]), device_id_type=MESH)
        copies[i] = c
        c.start()

    def advance(r, s, k):
        order = lanes[s]
        while k < len(order) and not r >> order[k] & 1:
            i = slots[order[k], r, s]
            copies[i].wait_recv()
            acc[r, s] += rcv[i]
            k += 1
        if k < len(order):
            exchange(order[k], r, s)

    def core_sum(r, s):
        i = slots[0, r, s]
        copies[i].wait_recv()
        acc[r, s] += rcv[i]
        if first(r, s) == 0:
            advance(r, s, 0)

    waited = False
    for at, (r, s) in enumerate(items):
        piece(r | 1, s)
        if not waited:
            pl.semaphore_wait(barrier, n + rows - 2)
            waited = True
        exchange(0, r | 1, s)
        piece(r, s)
        if at >= LAG:
            core_sum(*items[at - LAG])

    ones = jnp.ones((8, cols), jnp.bfloat16)
    counts = jnp.dot(ones, oh[...], preferred_element_type=jnp.float32)
    back = jnp.sum(totals[1], axis=0, keepdims=True)
    back = back + pltpu.roll(jnp.broadcast_to(back, (8, LANES)), CLUSTERS, 1)[0:1]
    tot[...] = jnp.concatenate([
        jnp.sum(totals[0], axis=0, keepdims=True), back,
        counts[0:1, :LANES], counts[0:1, LANES:] + pltpu.roll(counts[:, LANES:], CLUSTERS, 1)[0:1],
        jnp.zeros((4, LANES), jnp.float32)], axis=0)
    small = []
    for r in range(1, n):
        c = pltpu.make_async_remote_copy(
            src_ref=tot, dst_ref=tot_col.at[r - 1], send_sem=tsend.at[r - 1], recv_sem=trecv.at[r - 1],
            device_id=(row, peers[r]), device_id_type=MESH)
        c.start()
        small.append(c)

    for at in range(max(len(items) - LAG, 0), len(items)):
        core_sum(*items[at])
    for r, s in items:
        if r and first(r, s) > 0:
            advance(r, s, 0)

    total = tot[...]
    for r in range(1, n):
        small[r - 1].wait_recv()
        total = total + tot_col[r - 1]
    tot_sum[...] = total
    wide = []
    for d in range(1, rows):
        c = pltpu.make_async_remote_copy(
            src_ref=tot_sum, dst_ref=tot_row.at[d - 1], send_sem=rsend.at[d - 1], recv_sem=rrecv.at[d - 1],
            device_id=(lax.rem(row + d, rows), me), device_id_type=MESH)
        c.start()
        wide.append(c)
    for d in range(1, rows):
        wide[d - 1].wait_recv()
        total = total + tot_row[d - 1]

    total_of = total[0:2]
    count = total[2:4] / rows
    factor = -2.0 / count
    shift = total_of / (count * count)
    share = total_of / count
    left = lax.broadcasted_iota(jnp.int32, (1, LANES), 1) < CLUSTERS
    for t in range(iters):
        keep = left if t % 2 == 0 else jnp.logical_not(left)
        obj_ref[t] = 1.0 - jnp.sum(jnp.where(keep, share[t // 2:t // 2 + 1], 0.0)) / series

    for s in range(SPLITS):
        advance(0, s, 0)
        front = acc[0, s, :pr, :] * factor[0:1] + shift[0:1]
        back = acc[0, s, pr:, :] * factor[1:2] + shift[1:2]
        dist_ref[0, pl.ds(s * pr, pr), :] = front[:, :CLUSTERS]
        dist_ref[1, pl.ds(s * pr, pr), :] = front[:, CLUSTERS:]
        dist_ref[2, pl.ds(s * pr, half), :] = back[:, :CLUSTERS]
        dist_ref[2, pl.ds(s * pr + half, half), :] = back[:, CLUSTERS:]

    for c in list(copies.values()) + small + wide:
        c.wait_send()


def shards(n, rows, kernel, labels):
    rows_block, cols = kernel.shape
    iters, series = labels.shape
    slice_rows = rows_block // n
    pr = slice_rows // SPLITS
    packed = pr + pr // 2
    moves = SPLITS * (n - 1)
    f32 = jnp.float32
    return pl.pallas_call(
        functools.partial(body, n, rows, iters, series),
        out_shape=(jax.ShapeDtypeStruct((iters, slice_rows, CLUSTERS), f32), jax.ShapeDtypeStruct((iters,), f32)),
        in_specs=[pl.BlockSpec(memory_space=pl.ANY)] * 2,
        out_specs=(pl.BlockSpec(memory_space=pltpu.VMEM), pl.BlockSpec(memory_space=pltpu.SMEM)),
        scratch_shapes=[
            pltpu.VMEM((n, SPLITS, pr, cols), jnp.bfloat16),
            pltpu.VMEM((iters, cols), jnp.int32),
            pltpu.VMEM((n, iters, slice_rows), jnp.int32),
            pltpu.VMEM((cols, 2 * LANES), jnp.bfloat16),
            pltpu.VMEM((n, SPLITS, packed, LANES), f32),
            pltpu.VMEM((moves, packed, LANES), f32),
            pltpu.VMEM((8, LANES), f32),
            pltpu.VMEM((n - 1, 8, LANES), f32),
            pltpu.VMEM((8, LANES), f32),
            pltpu.VMEM((rows - 1, 8, LANES), f32),
            pltpu.SemaphoreType.DMA((n, SPLITS)),
            pltpu.SemaphoreType.DMA((n + 1,)),
            pltpu.SemaphoreType.DMA((moves,)),
            pltpu.SemaphoreType.DMA((moves,)),
            pltpu.SemaphoreType.DMA((n - 1,)),
            pltpu.SemaphoreType.DMA((n - 1,)),
            pltpu.SemaphoreType.DMA((rows - 1,)),
            pltpu.SemaphoreType.DMA((rows - 1,)),
        ],
        compiler_params=pltpu.CompilerParams(
            collective_id=0, has_side_effects=True, vmem_limit_bytes=60000 * 1024),
    )(kernel, labels)


def solution(mesh):
    return jax.shard_map(
        functools.partial(shards, mesh.shape["col"], mesh.shape["row"]),
        mesh=mesh,
        in_specs=(P("row", "col"), P()),
        out_specs=(P(None, ("row", "col"), None), P()),
        check_vma=False,
    )
```

```python
import functools

import jax
import jax.numpy as jnp
from jax import lax
from jax.experimental import pallas as pl
from jax.experimental.pallas import tpu as pltpu
from jax.sharding import PartitionSpec as P

CLUSTERS = 64
LANES = 128
SPLITS = 2
LAG = 1
AHEAD = 3
MESH = pl.DeviceIdType.MESH


def flip(index, mask, bits):
    out = 0
    for b in range(bits):
        bit = lax.rem(lax.div(index, 1 << b), 2)
        if mask >> b & 1:
            bit = 1 - bit
        out = out + bit * (1 << b)
    return out


def body(n, rows, iters, k_hbm, lab_hbm, sum_ref, tot_ref,
         kbuf, labc, labr, oh, acc, rcv, tot, tot_col, tot_sum, tot_row,
         k_sem, lab_sem, send_sem, recv_sem, tsend, trecv, rsend, rrecv):
    bits = n.bit_length() - 1
    pr = kbuf.shape[2]
    half = pr // 2
    cols = kbuf.shape[3]
    slice_rows = SPLITS * pr
    row = lax.axis_index("row")
    me = lax.axis_index("col")
    peers = [flip(me, r, bits) for r in range(n)]
    lanes = []
    for s in range(SPLITS):
        rest = list(range(1, bits))
        lanes.append(rest if s % 2 == 0 else rest[::-1])

    def first(r, s):
        hits = [k for k, b in enumerate(lanes[s]) if r >> b & 1]
        return hits[0] if hits else bits

    items = [(r, s) for r in range(0, n, 2) for s in range(SPLITS)]
    items.sort(key=lambda rs: (first(*rs), -bin(rs[0]).count("1"), rs[1]))

    slots = {}
    for s in range(SPLITS):
        gone = 0
        for b in [0] + lanes[s]:
            gone |= 1 << b
            for r in range(n):
                if r & gone == 0:
                    slots[b, r, s] = len(slots)

    lab_copies = [pltpu.make_async_copy(
        lab_hbm.at[:, pl.ds(pl.multiple_of(me * cols, LANES), cols)], labc, lab_sem.at[n])]
    lab_copies[0].start()
    k_copies = {}

    def fetch(r, s):
        start = peers[r] * slice_rows + s * pr
        k_copies[r, s] = pltpu.make_async_copy(
            k_hbm.at[pl.ds(pl.multiple_of(start, 16), pr), :], kbuf.at[r, s], k_sem.at[r, s])
        k_copies[r, s].start()

    queue = [(r | e, s) for r, s in items for e in (1, 0)]
    for at in queue[:AHEAD]:
        fetch(*at)
    queue = queue[AHEAD:]

    for r in range(0, n, 2):
        base = row * (n * slice_rows) + peers[r] * slice_rows
        lab_copies.append(pltpu.make_async_copy(
            lab_hbm.at[:, pl.ds(pl.multiple_of(base, LANES), slice_rows)], labr.at[r // 2], lab_sem.at[r]))
        lab_copies[-1].start()

    barrier = pltpu.get_barrier_semaphore()
    for r in range(1, n):
        pl.semaphore_signal(barrier, inc=1, device_id=(row, peers[r]), device_id_type=MESH)
    for d in range(1, rows):
        pl.semaphore_signal(barrier, inc=1, device_id=(lax.rem(row + d, rows), me), device_id_type=MESH)

    lab_copies[0].wait()
    width = oh.shape[1]
    step = 256
    for kb in range(cols // step):
        lab = labc[:, pl.ds(kb * step, step)]
        ids = lax.broadcasted_iota(jnp.int32, (CLUSTERS, step), 0)
        parts = [(ids == lab[t:t + 1, :]).astype(jnp.float32) for t in range(iters)]
        parts.append(jnp.zeros((width - iters * CLUSTERS, step), jnp.float32))
        oh[pl.ds(kb * step, step), :] = jnp.concatenate(parts, axis=0).T.astype(jnp.bfloat16)

    lane = lax.broadcasted_iota(jnp.int32, (pr, LANES), 1)
    low = lane < CLUSTERS
    totals = [jnp.zeros((8, LANES), jnp.float32) for _ in range(2)]

    def piece(r, s):
        k_copies[r, s].wait()
        if queue:
            fetch(*queue.pop(0))
        out = jnp.dot(kbuf[r, s], oh[...], preferred_element_type=jnp.float32)
        front, back = out[:, :LANES], out[:, LANES:]
        back = jnp.where(low[:half], back[:half], pltpu.roll(back[half:], CLUSTERS, 1))
        acc[r, s, :pr, :] = front
        acc[r, s, pr:, :] = back

    def add_totals(r, s):
        front, back = acc[r, s, :pr, :], acc[r, s, pr:, :]
        lab = labr[r // 2, :, s * pr:(s + 1) * pr]
        ids = lax.broadcasted_iota(jnp.int32, (CLUSTERS, pr), 0)
        hot = [(ids == lab[t:t + 1]).astype(jnp.float32) for t in range(iters)]
        mine = jnp.concatenate(hot[:2], axis=0).T
        totals[0] += jnp.sum((mine * front).reshape(pr // 8, 8, LANES), axis=0)
        mine = jnp.concatenate([hot[2][:, :half], hot[2][:, half:]], axis=0).T
        totals[1] += jnp.sum((mine * back).reshape(half // 8, 8, LANES), axis=0)

    copies = {}

    def exchange(b, r, s):
        i = slots[b, r & ~(1 << b), s]
        c = pltpu.make_async_remote_copy(
            src_ref=acc.at[r, s], dst_ref=rcv.at[i], send_sem=send_sem.at[i], recv_sem=recv_sem.at[i],
            device_id=(row, peers[1 << b]), device_id_type=MESH)
        copies[i] = c
        c.start()

    def advance(r, s, k):
        order = lanes[s]
        while k < len(order) and not r >> order[k] & 1:
            i = slots[order[k], r, s]
            copies[i].wait_recv()
            acc[r, s] += rcv[i]
            k += 1
        if k < len(order):
            exchange(order[k], r, s)

    def core_sum(r, s):
        i = slots[0, r, s]
        copies[i].wait_recv()
        acc[r, s] += rcv[i]
        if first(r, s) == 0:
            advance(r, s, 0)

    waited = False
    for at, (r, s) in enumerate(items):
        piece(r | 1, s)
        if not waited:
            pl.semaphore_wait(barrier, n + rows - 2)
            waited = True
        exchange(0, r | 1, s)
        piece(r, s)
        if at >= LAG:
            core_sum(*items[at - LAG])

    for at in range(max(len(items) - LAG, 0), len(items)):
        core_sum(*items[at])
    for c in lab_copies[1:]:
        c.wait()
    for r, s in items:
        add_totals(r, s)

    ones = jnp.ones((8, cols), jnp.bfloat16)
    counts = jnp.dot(ones, oh[...], preferred_element_type=jnp.float32)
    back = jnp.sum(totals[1], axis=0, keepdims=True)
    back = back + pltpu.roll(jnp.broadcast_to(back, (8, LANES)), CLUSTERS, 1)[0:1]
    tot[...] = jnp.concatenate([
        jnp.sum(totals[0], axis=0, keepdims=True), back,
        counts[0:1, :LANES], counts[0:1, LANES:] + pltpu.roll(counts[:, LANES:], CLUSTERS, 1)[0:1],
        jnp.zeros((4, LANES), jnp.float32)], axis=0)
    small = []
    for r in range(1, n):
        c = pltpu.make_async_remote_copy(
            src_ref=tot, dst_ref=tot_col.at[r - 1], send_sem=tsend.at[r - 1], recv_sem=trecv.at[r - 1],
            device_id=(row, peers[r]), device_id_type=MESH)
        c.start()
        small.append(c)

    for r, s in items:
        if r and first(r, s) > 0:
            advance(r, s, 0)

    total = tot[...]
    for r in range(1, n):
        small[r - 1].wait_recv()
        total = total + tot_col[r - 1]
    tot_sum[...] = total
    wide = []
    for d in range(1, rows):
        c = pltpu.make_async_remote_copy(
            src_ref=tot_sum, dst_ref=tot_row.at[d - 1], send_sem=rsend.at[d - 1], recv_sem=rrecv.at[d - 1],
            device_id=(lax.rem(row + d, rows), me), device_id_type=MESH)
        c.start()
        wide.append(c)
    for d in range(1, rows):
        wide[d - 1].wait_recv()
        total = total + tot_row[d - 1]

    tot_ref[...] = total
    for s in range(SPLITS):
        for k, b in enumerate(lanes[s]):
            i = slots[b, 0, s]
            copies[i].wait_recv()
            if k == len(lanes[s]) - 1:
                sum_ref[s] = acc[0, s] + rcv[i]
            else:
                acc[0, s] += rcv[i]

    for c in list(copies.values()) + small + wide:
        c.wait_send()


def finish(rows, series, sum_ref, tot_ref, dist_ref, obj_ref):
    total_of = tot_ref[0:2]
    count = tot_ref[2:4] / rows
    factor = -2.0 / count
    shift = total_of / (count * count)
    share = total_of / count
    left = lax.broadcasted_iota(jnp.int32, (1, LANES), 1) < CLUSTERS
    for t in range(obj_ref.shape[0]):
        keep = left if t % 2 == 0 else jnp.logical_not(left)
        obj_ref[t] = 1.0 - jnp.sum(jnp.where(keep, share[t // 2:t // 2 + 1], 0.0)) / series
    pr = sum_ref.shape[1] * 2 // 3
    half = pr // 2
    for s in range(SPLITS):
        front = (sum_ref[s, :pr, :] * factor[0:1] + shift[0:1]).T
        back = (sum_ref[s, pr:, :] * factor[1:2] + shift[1:2]).T
        dist_ref[0, :, s * pr:(s + 1) * pr] = front[:CLUSTERS]
        dist_ref[1, :, s * pr:(s + 1) * pr] = front[CLUSTERS:]
        dist_ref[2, :, s * pr:s * pr + half] = back[:CLUSTERS]
        dist_ref[2, :, s * pr + half:(s + 1) * pr] = back[CLUSTERS:]


def shards(n, rows, kernel, labels):
    rows_block, cols = kernel.shape
    iters, series = labels.shape
    slice_rows = rows_block // n
    pr = slice_rows // SPLITS
    packed = pr + pr // 2
    moves = SPLITS * (n - 1)
    f32 = jnp.float32
    sums, totals = pl.pallas_call(
        functools.partial(body, n, rows, iters),
        out_shape=(jax.ShapeDtypeStruct((SPLITS, packed, LANES), f32), jax.ShapeDtypeStruct((8, LANES), f32)),
        in_specs=[pl.BlockSpec(memory_space=pl.ANY)] * 2,
        out_specs=(pl.BlockSpec(memory_space=pltpu.VMEM),) * 2,
        scratch_shapes=[
            pltpu.VMEM((n, SPLITS, pr, cols), jnp.bfloat16),
            pltpu.VMEM((iters, cols), jnp.int32),
            pltpu.VMEM((n // 2, iters, slice_rows), jnp.int32),
            pltpu.VMEM((cols, 2 * LANES), jnp.bfloat16),
            pltpu.VMEM((n, SPLITS, packed, LANES), f32),
            pltpu.VMEM((moves, packed, LANES), f32),
            pltpu.VMEM((8, LANES), f32),
            pltpu.VMEM((n - 1, 8, LANES), f32),
            pltpu.VMEM((8, LANES), f32),
            pltpu.VMEM((rows - 1, 8, LANES), f32),
            pltpu.SemaphoreType.DMA((n, SPLITS)),
            pltpu.SemaphoreType.DMA((n + 1,)),
            pltpu.SemaphoreType.DMA((moves,)),
            pltpu.SemaphoreType.DMA((moves,)),
            pltpu.SemaphoreType.DMA((n - 1,)),
            pltpu.SemaphoreType.DMA((n - 1,)),
            pltpu.SemaphoreType.DMA((rows - 1,)),
            pltpu.SemaphoreType.DMA((rows - 1,)),
        ],
        compiler_params=pltpu.CompilerParams(
            collective_id=0, has_side_effects=True, vmem_limit_bytes=60000 * 1024),
    )(kernel, labels)
    distance, objective = pl.pallas_call(
        functools.partial(finish, rows, series),
        out_shape=(jax.ShapeDtypeStruct((iters, CLUSTERS, slice_rows), f32), jax.ShapeDtypeStruct((iters,), f32)),
        in_specs=[pl.BlockSpec(memory_space=pltpu.VMEM)] * 2,
        out_specs=(pl.BlockSpec(memory_space=pltpu.VMEM), pl.BlockSpec(memory_space=pltpu.SMEM)),
    )(sums, totals)
    return distance.transpose(0, 2, 1), objective


def solution(mesh):
    return jax.shard_map(
        functools.partial(shards, mesh.shape["col"], mesh.shape["row"]),
        mesh=mesh,
        in_specs=(P("row", "col"), P()),
        out_specs=(P(None, ("row", "col"), None), P()),
        check_vma=False,
    )
```

```python
import functools

import jax
import jax.numpy as jnp
from jax import lax
from jax.experimental import pallas as pl
from jax.experimental.pallas import tpu as pltpu
from jax.sharding import PartitionSpec as P

CLUSTERS = 64
LANES = 128
SPLITS = 2
LAG = 1
AHEAD = 3
MESH = pl.DeviceIdType.MESH


def flip(index, mask, bits):
    out = 0
    for b in range(bits):
        bit = lax.rem(lax.div(index, 1 << b), 2)
        if mask >> b & 1:
            bit = 1 - bit
        out = out + bit * (1 << b)
    return out


def body(n, rows, iters, k_hbm, lab_hbm, sum_ref, tot_ref,
         kbuf, labc, labr, oh, acc, rcv, tot, tot_col, tot_sum, tot_row,
         k_sem, lab_sem, send_sem, recv_sem, tsend, trecv, rsend, rrecv):
    bits = n.bit_length() - 1
    pr = kbuf.shape[2]
    half = pr // 2
    cols = kbuf.shape[3]
    slice_rows = SPLITS * pr
    row = lax.axis_index("row")
    me = lax.axis_index("col")
    peers = [flip(me, r, bits) for r in range(n)]
    lanes = []
    for s in range(SPLITS):
        rest = list(range(1, bits))
        lanes.append(rest if s % 2 == 0 else rest[::-1])

    def first(r, s):
        hits = [k for k, b in enumerate(lanes[s]) if r >> b & 1]
        return hits[0] if hits else bits

    items = [(r, s) for r in range(0, n, 2) for s in range(SPLITS)]
    items.sort(key=lambda rs: (first(*rs), -bin(rs[0]).count("1"), rs[1]))

    slots = {}
    for s in range(SPLITS):
        gone = 0
        for b in [0] + lanes[s]:
            gone |= 1 << b
            for r in range(n):
                if r & gone == 0:
                    slots[b, r, s] = len(slots)

    lab_copies = [pltpu.make_async_copy(
        lab_hbm.at[:, pl.ds(pl.multiple_of(me * cols, LANES), cols)], labc, lab_sem.at[n])]
    lab_copies[0].start()
    k_copies = {}

    def fetch(r, s):
        start = peers[r] * slice_rows + s * pr
        k_copies[r, s] = pltpu.make_async_copy(
            k_hbm.at[pl.ds(pl.multiple_of(start, 16), pr), :], kbuf.at[r, s], k_sem.at[r, s])
        k_copies[r, s].start()

    queue = [(r | e, s) for r, s in items for e in (1, 0)]
    for at in queue[:AHEAD]:
        fetch(*at)
    queue = queue[AHEAD:]

    for r in range(0, n, 2):
        base = row * (n * slice_rows) + peers[r] * slice_rows
        lab_copies.append(pltpu.make_async_copy(
            lab_hbm.at[:, pl.ds(pl.multiple_of(base, LANES), slice_rows)], labr.at[r // 2], lab_sem.at[r]))
        lab_copies[-1].start()

    barrier = pltpu.get_barrier_semaphore()
    for r in range(1, n):
        pl.semaphore_signal(barrier, inc=1, device_id=(row, peers[r]), device_id_type=MESH)
    for d in range(1, rows):
        pl.semaphore_signal(barrier, inc=1, device_id=(lax.rem(row + d, rows), me), device_id_type=MESH)

    lab_copies[0].wait()
    width = oh.shape[1]
    step = 256
    for kb in range(cols // step):
        lab = labc[:, pl.ds(kb * step, step)]
        ids = lax.broadcasted_iota(jnp.int32, (CLUSTERS, step), 0)
        parts = [(ids == lab[t:t + 1, :]).astype(jnp.float32) for t in range(iters)]
        parts.append(jnp.zeros((width - iters * CLUSTERS, step), jnp.float32))
        oh[pl.ds(kb * step, step), :] = jnp.concatenate(parts, axis=0).T.astype(jnp.bfloat16)

    lane = lax.broadcasted_iota(jnp.int32, (pr, LANES), 1)
    low = lane < CLUSTERS
    totals = [jnp.zeros((8, LANES), jnp.float32) for _ in range(2)]

    def piece(r, s):
        k_copies[r, s].wait()
        if queue:
            fetch(*queue.pop(0))
        out = jnp.dot(kbuf[r, s], oh[...], preferred_element_type=jnp.float32)
        front, back = out[:, :LANES], out[:, LANES:]
        back = jnp.where(low[:half], back[:half], pltpu.roll(back[half:], CLUSTERS, 1))
        acc[r, s, :pr, :] = front
        acc[r, s, pr:, :] = back

    def add_totals(r, s):
        front, back = acc[r, s, :pr, :], acc[r, s, pr:, :]
        lab = labr[r // 2, :, s * pr:(s + 1) * pr]
        ids = lax.broadcasted_iota(jnp.int32, (CLUSTERS, pr), 0)
        hot = [(ids == lab[t:t + 1]).astype(jnp.float32) for t in range(iters)]
        mine = jnp.concatenate(hot[:2], axis=0).T
        totals[0] += jnp.sum((mine * front).reshape(pr // 8, 8, LANES), axis=0)
        mine = jnp.concatenate([hot[2][:, :half], hot[2][:, half:]], axis=0).T
        totals[1] += jnp.sum((mine * back).reshape(half // 8, 8, LANES), axis=0)

    copies = {}

    def exchange(b, r, s):
        i = slots[b, r & ~(1 << b), s]
        c = pltpu.make_async_remote_copy(
            src_ref=acc.at[r, s], dst_ref=rcv.at[i], send_sem=send_sem.at[i], recv_sem=recv_sem.at[i],
            device_id=(row, peers[1 << b]), device_id_type=MESH)
        copies[i] = c
        c.start()

    def advance(r, s, k):
        order = lanes[s]
        while k < len(order) and not r >> order[k] & 1:
            i = slots[order[k], r, s]
            copies[i].wait_recv()
            acc[r, s] += rcv[i]
            k += 1
        if k < len(order):
            exchange(order[k], r, s)

    def core_sum(r, s):
        i = slots[0, r, s]
        copies[i].wait_recv()
        acc[r, s] += rcv[i]
        if first(r, s) == 0:
            advance(r, s, 0)

    waited = False
    for at, (r, s) in enumerate(items):
        piece(r | 1, s)
        if not waited:
            pl.semaphore_wait(barrier, n + rows - 2)
            waited = True
        exchange(0, r | 1, s)
        piece(r, s)
        if at >= LAG:
            core_sum(*items[at - LAG])

    for at in range(max(len(items) - LAG, 0), len(items)):
        core_sum(*items[at])
    for c in lab_copies[1:]:
        c.wait()
    for r, s in items:
        add_totals(r, s)

    ones = jnp.ones((8, cols), jnp.bfloat16)
    counts = jnp.dot(ones, oh[...], preferred_element_type=jnp.float32)
    back = jnp.sum(totals[1], axis=0, keepdims=True)
    back = back + pltpu.roll(jnp.broadcast_to(back, (8, LANES)), CLUSTERS, 1)[0:1]
    tot[...] = jnp.concatenate([
        jnp.sum(totals[0], axis=0, keepdims=True), back,
        counts[0:1, :LANES], counts[0:1, LANES:] + pltpu.roll(counts[:, LANES:], CLUSTERS, 1)[0:1],
        jnp.zeros((4, LANES), jnp.float32)], axis=0)
    small = []
    for r in range(1, n):
        c = pltpu.make_async_remote_copy(
            src_ref=tot, dst_ref=tot_col.at[r - 1], send_sem=tsend.at[r - 1], recv_sem=trecv.at[r - 1],
            device_id=(row, peers[r]), device_id_type=MESH)
        c.start()
        small.append(c)

    for r, s in items:
        if r and first(r, s) > 0:
            advance(r, s, 0)

    total = tot[...]
    for r in range(1, n):
        small[r - 1].wait_recv()
        total = total + tot_col[r - 1]
    tot_sum[...] = total
    wide = []
    for d in range(1, rows):
        c = pltpu.make_async_remote_copy(
            src_ref=tot_sum, dst_ref=tot_row.at[d - 1], send_sem=rsend.at[d - 1], recv_sem=rrecv.at[d - 1],
            device_id=(lax.rem(row + d, rows), me), device_id_type=MESH)
        c.start()
        wide.append(c)
    for d in range(1, rows):
        wide[d - 1].wait_recv()
        total = total + tot_row[d - 1]

    tot_ref[...] = total
    for s in range(SPLITS):
        for k, b in enumerate(lanes[s]):
            i = slots[b, 0, s]
            copies[i].wait_recv()
            if k == len(lanes[s]) - 1:
                sum_ref[s] = acc[0, s] + rcv[i]
            else:
                acc[0, s] += rcv[i]

    for c in list(copies.values()) + small + wide:
        c.wait_send()


def finish(rows, series, sum_ref, tot_ref, dist_ref, obj_ref):
    total_of = tot_ref[0:2]
    count = tot_ref[2:4] / rows
    factor = -2.0 / count
    shift = total_of / (count * count)
    share = total_of / count
    left = lax.broadcasted_iota(jnp.int32, (1, LANES), 1) < CLUSTERS
    for t in range(obj_ref.shape[0]):
        keep = left if t % 2 == 0 else jnp.logical_not(left)
        obj_ref[t] = 1.0 - jnp.sum(jnp.where(keep, share[t // 2:t // 2 + 1], 0.0)) / series
    pr = sum_ref.shape[1] * 2 // 3
    half = pr // 2
    for s in range(SPLITS):
        front = (sum_ref[s, :pr, :] * factor[0:1] + shift[0:1]).T
        back = (sum_ref[s, pr:, :] * factor[1:2] + shift[1:2]).T
        dist_ref[0, :, s * pr:(s + 1) * pr] = front[:CLUSTERS]
        dist_ref[1, :, s * pr:(s + 1) * pr] = front[CLUSTERS:]
        dist_ref[2, :, s * pr:s * pr + half] = back[:CLUSTERS]
        dist_ref[2, :, s * pr + half:(s + 1) * pr] = back[CLUSTERS:]


def shards(n, rows, kernel, labels):
    rows_block, cols = kernel.shape
    iters, series = labels.shape
    slice_rows = rows_block // n
    pr = slice_rows // SPLITS
    packed = pr + pr // 2
    moves = SPLITS * (n - 1)
    f32 = jnp.float32
    sums, totals = pl.pallas_call(
        functools.partial(body, n, rows, iters),
        out_shape=(jax.ShapeDtypeStruct((SPLITS, packed, LANES), f32), jax.ShapeDtypeStruct((8, LANES), f32)),
        in_specs=[pl.BlockSpec(memory_space=pltpu.HBM)] * 2,
        out_specs=(pl.BlockSpec(memory_space=pltpu.VMEM),) * 2,
        scratch_shapes=[
            pltpu.VMEM((n, SPLITS, pr, cols), jnp.bfloat16),
            pltpu.VMEM((iters, cols), jnp.int32),
            pltpu.VMEM((n // 2, iters, slice_rows), jnp.int32),
            pltpu.VMEM((cols, 2 * LANES), jnp.bfloat16),
            pltpu.VMEM((n, SPLITS, packed, LANES), f32),
            pltpu.VMEM((moves, packed, LANES), f32),
            pltpu.VMEM((8, LANES), f32),
            pltpu.VMEM((n - 1, 8, LANES), f32),
            pltpu.VMEM((8, LANES), f32),
            pltpu.VMEM((rows - 1, 8, LANES), f32),
            pltpu.SemaphoreType.DMA((n, SPLITS)),
            pltpu.SemaphoreType.DMA((n + 1,)),
            pltpu.SemaphoreType.DMA((moves,)),
            pltpu.SemaphoreType.DMA((moves,)),
            pltpu.SemaphoreType.DMA((n - 1,)),
            pltpu.SemaphoreType.DMA((n - 1,)),
            pltpu.SemaphoreType.DMA((rows - 1,)),
            pltpu.SemaphoreType.DMA((rows - 1,)),
        ],
        compiler_params=pltpu.CompilerParams(
            collective_id=0, has_side_effects=True, vmem_limit_bytes=50000 * 1024),
    )(*[pltpu.with_memory_space_constraint(v, pltpu.HBM) for v in (kernel, labels)])
    distance, objective = pl.pallas_call(
        functools.partial(finish, rows, series),
        out_shape=(jax.ShapeDtypeStruct((iters, CLUSTERS, slice_rows), f32), jax.ShapeDtypeStruct((iters,), f32)),
        in_specs=[pl.BlockSpec(memory_space=pltpu.VMEM)] * 2,
        out_specs=(pl.BlockSpec(memory_space=pltpu.VMEM), pl.BlockSpec(memory_space=pltpu.SMEM)),
        compiler_params=pltpu.CompilerParams(vmem_limit_bytes=8192 * 1024),
    )(sums, totals)
    return distance.transpose(0, 2, 1), objective


def solution(mesh):
    return jax.shard_map(
        functools.partial(shards, mesh.shape["col"], mesh.shape["row"]),
        mesh=mesh,
        in_specs=(P("row", "col"), P()),
        out_specs=(P(None, ("row", "col"), None), P()),
        check_vma=False,
    )
```
